32 devices in a mesh: tm: 4 (over z), height: 4 (over y, core), heads: 2 (over x).
Axes of the slice: x: 2, y: 2, z: 4, core: 2. Of those that a mesh axis runs over, the one named last changes fastest.
Arguments:
- grad_output: bfloat16 [4, 4, 384, 3072], P('tm', 'height', None, 'heads'), may hold values from -6 to 6
- out_weight: bfloat16 [2048, 3072], P(None, 'heads'), may hold values from -0.109375 to 0.109375
- queries: bfloat16 [4, 4, 384, 2048], P('tm', 'height', None, 'heads'), may hold values from -24 to 24
- key_states: bfloat16 [4, 4, 384, 2048], P('tm', 'height', None, 'heads'), may hold values from -4 to 4
- value_states: bfloat16 [4, 4, 384, 2048], P('tm', 'height', None, 'heads'), may hold values from -6 to 6
- window: int32 [4, 4, 1, 27], replicated, may hold values from 0 to 1, as said below
Outputs:
- query_grad: bfloat16 [4, 4, 384, 2048], P('tm', 'height', None, 'heads')
- key_grad: bfloat16 [4, 4, 384, 2048], P('tm', 'height', None, 'heads')
- value_grad: bfloat16 [4, 4, 384, 2048], P('tm', 'height', None, 'heads')
The draws below stay inside these ranges and needn't reach their ends.
Inputs may be any that keep to these rules, and one draw needn't show every extreme that they name: window[t, h, w, 9(a+1) + 3(b+1) + (c+1)] is 1 where query tile (t, h, w) attends key tile (t+a, h+b, w+c), a, b, c each -1, 0 or 1; it is 1 at index 13 (the tile itself) and 0 where the key tile lies outside the video.
All inputs are finite; a program needn't handle non-finite values.
Results may differ from the reference program's by a relative error of at most 0.02.
Values may be sent and summed in bfloat16 or wider, within the bound.
No kernel may reach another device: no remote copies, remote signals or barrier semaphores. Data moves between devices by JAX's collectives and lax.ppermute only.
A program may use at most 128 MiB of HBM per device.

```python
import jax
import jax.numpy as jnp
from jax import lax

D = 3072
HEADS = 16
HD = 128
TILE = 384
TW = 1
TT = 4
TH = 4
DCHUNK = 1536
N_HEADS = 2


def draw_both(key):
    tokens = TW * TILE
    shape = (TT, TH, tokens, HEADS * HD)
    base_key = jax.random.fold_in(key, 71)
    first_key, second_key = jax.random.split(base_key)
    keys_drawn = jnp.clip(jax.random.normal(first_key, shape, jnp.float32), -4.0, 4.0)
    queries_drawn = jnp.clip(jax.random.normal(second_key, shape, jnp.float32), -4.0, 4.0)
    return (queries_drawn, keys_drawn)


def draw_queries(key, part):
    queries_drawn, keys_drawn = draw_both(key)
    return queries_drawn.astype(jnp.bfloat16)


def draw_key_states(key, part):
    queries_drawn, keys_drawn = draw_both(key)
    return keys_drawn.astype(jnp.bfloat16)


def draw_window(key, part):
    base_key = jax.random.fold_in(key, 13)
    level_key, roll_key = jax.random.split(base_key)
    ladder = jax.random.randint(level_key, (TT, TH, 1, 1), 0, 4)
    levels = ladder * ladder
    rolled = jax.random.randint(roll_key, (TT, TH, TW, 27), 0, 16)
    offset = jnp.arange(27)
    time_pos = jnp.arange(TT)[:, None, None, None] + (offset // 9 - 1)[None, None, None, :]
    height_pos = jnp.arange(TH)[None, :, None, None] + (offset // 3 % 3 - 1)[None, None, None, :]
    width_pos = jnp.arange(TW)[None, None, :, None] + (offset % 3 - 1)[None, None, None, :]
    inside = (time_pos >= 0) & (time_pos < TT) & (height_pos >= 0) & (height_pos < TH) & (width_pos >= 0) & (width_pos < TW)
    active = ((rolled < levels) | (offset == 13)[None, None, None, :]) & inside
    return active.astype(jnp.int32)


def level_of(rng, extent, cuts, low, high):
    factor_of, own = 1.0, jax.random.fold_in(rng, 6)
    for dim, blocks in cuts:
        heights = jnp.exp(jax.random.uniform(jax.random.fold_in(own, dim), (blocks,), jnp.float32, low / len(cuts), high / len(cuts)))
        factor_of = factor_of * jnp.repeat(heights, extent[dim] // blocks).reshape([-1 if axis == dim else 1 for axis in range(len(extent))])
    return factor_of


def gaussian(rng, extent, deviation, bound, pieces=(), kind=jnp.bfloat16):
    values = jax.random.normal(rng, extent, jnp.float32) * deviation
    if len(pieces) > 0:
        values = level_of(rng, extent, pieces, -0.22, 0.18) * values
    return jnp.clip(values, min=-bound, max=bound).astype(kind)


def setup_inputs(seed: int = 0) -> dict:
    keys = jax.random.split(jax.random.key(seed), 7)
    grad_output = gaussian(keys[0], (TT, TH, TW * TILE, D), 1.0, 6.0, ((0, 4), (1, 4), (3, 2)))
    out_weight = gaussian(keys[1], (HEADS * HD, D), D ** -0.5, 0.109375, ((1, 2),))
    queries = draw_queries(jax.random.fold_in(keys[6], 71), 0)
    key_states = draw_key_states(jax.random.fold_in(keys[6], 71), 0)
    value_states = gaussian(keys[4], (TT, TH, TW * TILE, HEADS * HD), 1.0, 6.0, ((0, 4), (1, 4), (3, 2)))
    window = draw_window(jax.random.fold_in(keys[6], 71), 0)
    return dict(grad_output=grad_output, out_weight=out_weight, queries=queries, key_states=key_states, value_states=value_states, window=window)


lowest = -1.0e30


def rounded(values):
    return lax.optimization_barrier(values.astype(jnp.bfloat16)).astype(jnp.float32)


def neighbour(tile_index, offset, sign):
    time_pos = tile_index // (TH * TW) + sign * (offset // 9 - 1)
    height_pos = (tile_index // TW) % TH + sign * ((offset // 3) % 3 - 1)
    width_pos = tile_index % TW + sign * (offset % 3 - 1)
    inside = (time_pos >= 0) & (time_pos < TT) & (height_pos >= 0) & (height_pos < TH) & (width_pos >= 0) & (width_pos < TW)
    clipped = jnp.clip(time_pos, 0, TT - 1) * (TH * TW) + jnp.clip(height_pos, 0, TH - 1) * TW + jnp.clip(width_pos, 0, TW - 1)
    return inside, clipped.astype(jnp.int32)


def reference(grad_output, out_weight, queries, key_states, value_states, window):
    scaling = HD ** -0.5
    grad_rows = grad_output.reshape(-1, D)
    summed = jnp.zeros((grad_rows.shape[0], HEADS * HD), jnp.float32)
    for part in range(N_HEADS):
        term = lax.dot_general(grad_rows[:, part * DCHUNK:(part + 1) * DCHUNK], out_weight[:, part * DCHUNK:(part + 1) * DCHUNK], (((1,), (1,)), ((), ())), preferred_element_type=jnp.float32)
        summed = summed + rounded(term)
    tile_total = TT * TH * TW
    grad_tiles = summed.astype(jnp.bfloat16).reshape(tile_total, TILE, HEADS, HD)
    query_tiles = queries.reshape(tile_total, TILE, HEADS, HD)
    key_tiles = key_states.reshape(tile_total, TILE, HEADS, HD)
    value_tiles = value_states.reshape(tile_total, TILE, HEADS, HD)
    windows = window.reshape(tile_total, 27)
    indices = jnp.arange(tile_total, dtype=jnp.int32)
    offsets = jnp.arange(27, dtype=jnp.int32)

    def scores_of(query_index, key_index):
        query_tile = query_tiles[query_index].astype(jnp.float32)
        grad_tile = grad_tiles[query_index].astype(jnp.float32)
        key_tile = key_tiles[key_index].astype(jnp.float32)
        value_tile = value_tiles[key_index].astype(jnp.float32)
        scores = jnp.einsum("qhd,khd->hqk", query_tile, key_tile) * scaling
        slopes = jnp.einsum("qhd,khd->hqk", grad_tile, value_tile)
        return scores, slopes

    def tile_stats(query_index):
        def visit(carried, offset):
            inside, key_index = neighbour(query_index, offset, 1)
            active = inside & (windows[query_index, offset] == 1)

            def include(current):
                highest, totals, weighted = current
                scores, slopes = scores_of(query_index, key_index)
                renewed = jnp.maximum(highest, jnp.max(scores, axis=2))
                factor = jnp.exp(highest - renewed)
                weights = jnp.exp(scores - renewed[:, :, None])
                return renewed, totals * factor + jnp.sum(weights, axis=2), weighted * factor + jnp.sum(weights * slopes, axis=2)

            return lax.cond(active, include, lambda unchanged: unchanged, carried), None

        start_state = (jnp.full((HEADS, TILE), lowest, jnp.float32), jnp.zeros((HEADS, TILE), jnp.float32), jnp.zeros((HEADS, TILE), jnp.float32))
        final_state, unused = lax.scan(visit, start_state, offsets)
        highest, totals, weighted = final_state
        return highest + jnp.log(totals), weighted / totals

    log_totals, mean_slopes = lax.map(tile_stats, indices)

    def tile_query(query_index):
        def visit(running, offset):
            inside, key_index = neighbour(query_index, offset, 1)
            active = inside & (windows[query_index, offset] == 1)

            def include(previous):
                scores, slopes = scores_of(query_index, key_index)
                probabilities = jnp.exp(scores - log_totals[query_index][:, :, None])
                score_grads = rounded(probabilities * (slopes - mean_slopes[query_index][:, :, None]))
                return previous + jnp.einsum("hqk,khd->qhd", score_grads, key_tiles[key_index].astype(jnp.float32))

            return lax.cond(active, include, lambda unchanged: unchanged, running), None

        summed_grads, unused = lax.scan(visit, jnp.zeros((TILE, HEADS, HD), jnp.float32), offsets)
        return (scaling * summed_grads).astype(jnp.bfloat16)

    def tile_key(key_index):
        def visit(carried, offset):
            inside, query_index = neighbour(key_index, offset, -1)
            active = inside & (windows[query_index, offset] == 1)

            def include(previous):
                key_sum, value_sum = previous
                scores, slopes = scores_of(query_index, key_index)
                probabilities = jnp.exp(scores - log_totals[query_index][:, :, None])
                score_grads = rounded(probabilities * (slopes - mean_slopes[query_index][:, :, None]))
                value_sum = value_sum + jnp.einsum("hqk,qhd->khd", rounded(probabilities), grad_tiles[query_index].astype(jnp.float32))
                key_sum = key_sum + jnp.einsum("hqk,qhd->khd", score_grads, query_tiles[query_index].astype(jnp.float32))
                return key_sum, value_sum

            return lax.cond(active, include, lambda unchanged: unchanged, carried), None

        start_sums = (jnp.zeros((TILE, HEADS, HD), jnp.float32), jnp.zeros((TILE, HEADS, HD), jnp.float32))
        final_sums, unused = lax.scan(visit, start_sums, offsets)
        return (scaling * final_sums[0]).astype(jnp.bfloat16), final_sums[1].astype(jnp.bfloat16)

    query_grad = lax.map(tile_query, indices)
    key_grad, value_grad = lax.map(tile_key, indices)
    shape = (TT, TH, TW * TILE, HEADS * HD)
    return query_grad.reshape(shape), key_grad.reshape(shape), value_grad.reshape(shape)
```

```python
import functools

import jax
import jax.numpy as jnp
from jax import lax
from jax.experimental import pallas as pl
from jax.experimental.pallas import tpu as pltpu
from jax.sharding import PartitionSpec as P

HD = 128
LOG2E = 1.4426950408889634
NT = (((1,), (1,)), ((), ()))
TN = (((0,), (0,)), ((), ()))
CHUNK = 128


def params(limit=48 << 20):
    return pltpu.CompilerParams(vmem_limit_bytes=limit)


def vmem():
    return pl.BlockSpec(memory_space=pltpu.VMEM)


def smem():
    return pl.BlockSpec(memory_space=pltpu.SMEM)


def hbm():
    return pl.BlockSpec(memory_space=pl.ANY)


def split_kernel(count, me_ref, *refs):
    arrays = refs[:count]
    outs = refs[count:]
    pieces = len(outs) // count
    for index in range(count):
        width = arrays[index].shape[1] // pieces
        for slot in range(pieces):
            start = pl.multiple_of((me_ref[0] ^ slot) * width, width)
            outs[index * pieces + slot][...] = arrays[index][:, pl.ds(start, width)]


def split(arrays, me, pieces):
    rows, columns = arrays[0].shape
    out = jax.ShapeDtypeStruct((rows, columns // pieces), arrays[0].dtype)
    flat = pl.pallas_call(
        functools.partial(split_kernel, len(arrays)),
        out_shape=[out] * (len(arrays) * pieces),
        in_specs=[smem()] + [vmem()] * len(arrays),
        out_specs=[vmem()] * (len(arrays) * pieces),
        name="split_heads",
        cost_estimate=pl.CostEstimate(
            flops=0, transcendentals=0, bytes_accessed=4 * rows * columns * len(arrays)
        ),
    )(me, *arrays)
    return [flat[i * pieces : (i + 1) * pieces] for i in range(len(arrays))]


def join_kernel(me_ref, *refs):
    out = refs[-1]
    pieces = refs[:-1]
    width = pieces[0].shape[1]
    for slot, piece in enumerate(pieces):
        start = pl.multiple_of((me_ref[0] ^ slot) * width, width)
        out[:, pl.ds(start, width)] = piece[...]


def join(pieces, me):
    rows, width = pieces[0].shape
    columns = width * len(pieces)
    return pl.pallas_call(
        join_kernel,
        out_shape=jax.ShapeDtypeStruct((rows, columns), pieces[0].dtype),
        in_specs=[smem()] + [vmem()] * len(pieces),
        out_specs=vmem(),
        name="join_heads",
        cost_estimate=pl.CostEstimate(
            flops=0, transcendentals=0, bytes_accessed=4 * rows * columns
        ),
    )(me, *pieces)


def swap(pieces, count):
    return [pieces[0]] + [
        lax.ppermute(pieces[slot], "height", [(i, i ^ slot) for i in range(count)])
        for slot in range(1, count)
    ]


def project_kernel(base_ref, grad_ref, weight_ref, out_ref):
    out_ref[...] = lax.dot_general(
        grad_ref[...], weight_ref[...], NT, preferred_element_type=jnp.float32
    ).astype(out_ref.dtype)[None]


def project(grad_rows, weight, half, me, features, pieces):
    tokens, depth = grad_rows.shape
    width = features // pieces
    base = jnp.stack([half * pieces, me])
    return pl.pallas_call(
        project_kernel,
        out_shape=jax.ShapeDtypeStruct((pieces, tokens, width), jnp.bfloat16),
        grid_spec=pltpu.PrefetchScalarGridSpec(
            num_scalar_prefetch=1,
            grid=(pieces,),
            in_specs=[
                pl.BlockSpec((tokens, depth), lambda k, base: (0, 0)),
                pl.BlockSpec((width, depth), lambda k, base: (base[0] + (base[1] ^ k), 0)),
            ],
            out_specs=pl.BlockSpec((1, tokens, width), lambda k, base: (k, 0, 0)),
        ),
        compiler_params=params(),
        name="project",
        cost_estimate=pl.CostEstimate(
            flops=2 * tokens * depth * features,
            transcendentals=0,
            bytes_accessed=2 * features * depth,
        ),
    )(base, grad_rows, weight)


def add_kernel(mine_ref, other_ref, *outs):
    for slot, out in enumerate(outs):
        out[...] = (
            mine_ref[slot].astype(jnp.float32) + other_ref[slot].astype(jnp.float32)
        ).astype(out.dtype)


def add_parts(mine, other):
    pieces, rows, width = mine.shape
    out = jax.ShapeDtypeStruct((rows, width), mine.dtype)
    return pl.pallas_call(
        add_kernel,
        out_shape=[out] * pieces,
        in_specs=[vmem()] * 2,
        out_specs=[vmem()] * pieces,
        name="add_parts",
        cost_estimate=pl.CostEstimate(
            flops=pieces * rows * width,
            transcendentals=0,
            bytes_accessed=6 * pieces * rows * width,
        ),
    )(mine, other)


def total_kernel(own_ref, low_ref, high_ref, *outs):
    for slot, out in enumerate(outs):
        out[...] = (
            own_ref[slot]
            + (low_ref[slot].astype(jnp.float32) + high_ref[slot].astype(jnp.float32))
        ).astype(out.dtype)


def total(own, low, high):
    pieces, rows, width = own.shape
    out = jax.ShapeDtypeStruct((rows, width), low.dtype)
    return pl.pallas_call(
        total_kernel,
        out_shape=[out] * pieces,
        in_specs=[vmem()] * 3,
        out_specs=[vmem()] * pieces,
        name="total_grads",
        cost_estimate=pl.CostEstimate(
            flops=2 * pieces * rows * width,
            transcendentals=0,
            bytes_accessed=10 * pieces * rows * width,
        ),
    )(own, low, high)


def attend_kernel(rows_count, pos_ref, window_ref, *refs):
    q_in = refs[0:rows_count]
    g_in = refs[rows_count : 2 * rows_count]
    k_in = refs[2 * rows_count : 2 * rows_count + 3]
    v_in = refs[2 * rows_count + 3 : 2 * rows_count + 6]
    rest = refs[2 * rows_count + 6 :]
    dq_out, dk_own, dk_low, dk_high, dv_own, dv_low, dv_high = rest[:7]
    q_all, g_all, k_all, v_all, dk_acc, dv_acc, s_buf, d_buf, order, sem = rest[7:]
    head = pl.program_id(0)
    slot = pl.program_id(1)
    tile = q_all.shape[1]
    scaling = HD**-0.5
    chunks = [slice(c * CHUNK, (c + 1) * CHUNK) for c in range(tile // CHUNK)]
    time_index = pos_ref[0]
    me = pos_ref[1]

    @pl.when((head == 0) & (slot == 0))
    def _():
        copies = []
        for i in range(rows_count):
            copies.append(pltpu.make_async_copy(q_in[i], q_all.at[i], sem.at[i]))
            copies.append(pltpu.make_async_copy(g_in[i], g_all.at[i], sem.at[rows_count + i]))
        for i in range(3):
            part = pl.ds(i * rows_count, rows_count)
            copies.append(
                pltpu.make_async_copy(k_in[i], k_all.at[part], sem.at[2 * rows_count + i])
            )
            copies.append(
                pltpu.make_async_copy(v_in[i], v_all.at[part], sem.at[2 * rows_count + 3 + i])
            )
        for copy in copies:
            copy.start()
        for copy in copies:
            copy.wait()

    @pl.when(slot == 0)
    def _():
        dk_acc[...] = jnp.zeros_like(dk_acc)
        dv_acc[...] = jnp.zeros_like(dv_acc)

    row = me ^ slot
    base = (time_index * rows_count + row) * 27
    count = jnp.int32(0)
    for a in range(3):
        for b in range(3):
            flag = window_ref[base + 9 * a + 3 * b + 1]
            order[count] = a * rows_count + ((row + b - 1) ^ me)
            count = count + flag

    columns = pl.ds(pl.multiple_of(head * HD, HD), HD)
    query = q_all[slot, :, columns]
    grad = g_all[slot, :, columns]

    def scores(i, highest):
        key = k_all[order[i], :, columns]
        for part in chunks:
            s = lax.dot_general(key[part], query, NT, preferred_element_type=jnp.float32)
            s_buf[i, part, :] = s
            highest = jnp.maximum(highest, jnp.max(s.reshape(-1, 8, tile), axis=0))
        return highest

    highest = lax.fori_loop(0, count, scores, jnp.full((8, tile), -1e30, jnp.float32))
    highest = jnp.max(highest, axis=0, keepdims=True)
    factor = scaling * LOG2E

    def sums(i, carried):
        mass, weighted = carried
        value = v_all[order[i], :, columns]
        for part in chunks:
            slopes = lax.dot_general(value[part], grad, NT, preferred_element_type=jnp.float32)
            weights = jnp.exp2((s_buf[i, part, :] - highest) * factor)
            s_buf[i, part, :] = weights
            d_buf[i, part, :] = slopes
            mass = mass + jnp.sum(weights.reshape(-1, 8, tile), axis=0)
            weighted = weighted + jnp.sum((weights * slopes).reshape(-1, 8, tile), axis=0)
        return mass, weighted

    zero = jnp.zeros((8, tile), jnp.float32)
    mass, weighted = lax.fori_loop(0, count, sums, (zero, zero))
    mass = jnp.sum(mass, axis=0, keepdims=True)
    weighted = jnp.sum(weighted, axis=0, keepdims=True)
    inverse = 1.0 / mass
    delta = weighted * inverse

    def grads(i, query_sum):
        where = order[i]
        key = k_all[where, :, columns]
        for part in chunks:
            weights = s_buf[i, part, :] * inverse
            slopes = (weights * (d_buf[i, part, :] - delta)).astype(jnp.bfloat16)
            weights = weights.astype(jnp.bfloat16)
            dv_acc[where, part, :] += jnp.dot(weights, grad, preferred_element_type=jnp.float32)
            dk_acc[where, part, :] += jnp.dot(slopes, query, preferred_element_type=jnp.float32)
            query_sum = query_sum + lax.dot_general(
                key[part], slopes, TN, preferred_element_type=jnp.float32
            )
        return query_sum

    query_sum = lax.fori_loop(0, count, grads, jnp.zeros((HD, tile), jnp.float32))
    dq_out[0] = (scaling * query_sum).T.astype(dq_out.dtype)

    @pl.when(slot == rows_count - 1)
    def _():
        low, own, high = [pl.ds(i * rows_count, rows_count) for i in range(3)]
        dk_low[...] = (scaling * dk_acc[low]).astype(dk_low.dtype)
        dk_own[...] = scaling * dk_acc[own]
        dk_high[...] = (scaling * dk_acc[high]).astype(dk_high.dtype)
        dv_low[...] = dv_acc[low].astype(dv_low.dtype)
        dv_own[...] = dv_acc[own]
        dv_high[...] = dv_acc[high].astype(dv_high.dtype)


def attend(q_pieces, g_pieces, k_three, v_three, position, window):
    rows_count = len(q_pieces)
    tile, width = q_pieces[0].shape
    heads_here = width // HD
    stack = (rows_count, tile, width)
    bf16, f32 = jnp.bfloat16, jnp.float32
    kinds = [bf16, f32, bf16, bf16, f32, bf16, bf16]
    whole_block = pl.BlockSpec((rows_count, tile, HD), lambda n, k, *_: (0, 0, n))
    pairs = 9
    flops = heads_here * rows_count * 3 * 10 * tile * tile * HD
    return pl.pallas_call(
        functools.partial(attend_kernel, rows_count),
        out_shape=[jax.ShapeDtypeStruct(stack, kind) for kind in kinds],
        grid_spec=pltpu.PrefetchScalarGridSpec(
            num_scalar_prefetch=2,
            grid=(heads_here, rows_count),
            in_specs=[hbm()] * (2 * rows_count + 6),
            out_specs=[pl.BlockSpec((1, tile, HD), lambda n, k, *_: (k, 0, n))]
            + [whole_block] * 6,
            scratch_shapes=[
                pltpu.VMEM(stack, bf16),
                pltpu.VMEM(stack, bf16),
                pltpu.VMEM((3 * rows_count, tile, width), bf16),
                pltpu.VMEM((3 * rows_count, tile, width), bf16),
                pltpu.VMEM((3 * rows_count, tile, HD), f32),
                pltpu.VMEM((3 * rows_count, tile, HD), f32),
                pltpu.VMEM((pairs, tile, tile), f32),
                pltpu.VMEM((pairs, tile, tile), f32),
                pltpu.SMEM((16,), jnp.int32),
                pltpu.SemaphoreType.DMA((2 * rows_count + 6,)),
            ],
        ),
        compiler_params=params(),
        name="attend",
        cost_estimate=pl.CostEstimate(
            flops=flops, transcendentals=flops // (10 * HD), bytes_accessed=20 * tile * width * 4
        ),
    )(position, window, *q_pieces, *g_pieces, *k_three, *v_three)


def fast_body(grad_output, out_weight, queries, key_states, value_states, window):
    tokens, features = queries.shape[2], queries.shape[3]
    height_count = lax.axis_size("height")
    time_count = lax.axis_size("tm")
    me = lax.axis_index("height").astype(jnp.int32)
    time_index = lax.axis_index("tm").astype(jnp.int32)
    side = lax.axis_index("heads").astype(jnp.int32)
    me_array = me.reshape(1)
    up = [(i, i + 1) for i in range(time_count - 1)]
    down = [(i + 1, i) for i in range(time_count - 1)]

    grad_rows = grad_output.reshape(tokens, -1)
    query_rows = queries.reshape(tokens, features)
    key_rows = key_states.reshape(tokens, features)
    value_rows = value_states.reshape(tokens, features)

    (key_pieces,) = split([key_rows], me_array, height_count)
    key_stack = jnp.stack(swap(key_pieces, height_count))
    away = project(grad_rows, out_weight, 1 - side, me, features, height_count)
    arrived = lax.ppermute(away, "heads", [(0, 1), (1, 0)])
    value_pieces, query_pieces = split([value_rows, query_rows], me_array, height_count)
    value_stack = jnp.stack(swap(value_pieces, height_count))
    key_low = lax.ppermute(key_stack, "tm", up)
    key_high = lax.ppermute(key_stack, "tm", down)
    query_pieces = swap(query_pieces, height_count)
    mine = project(grad_rows, out_weight, side, me, features, height_count)
    value_low = lax.ppermute(value_stack, "tm", up)
    value_high = lax.ppermute(value_stack, "tm", down)
    grad_pieces = swap(add_parts(mine, arrived), height_count)

    position = jnp.stack([time_index, me])
    dq, dk_own, dk_low, dk_high, dv_own, dv_low, dv_high = attend(
        query_pieces,
        grad_pieces,
        [key_low, key_stack, key_high],
        [value_low, value_stack, value_high],
        position,
        window.reshape(-1),
    )
    shape = (1, 1, tokens, features)

    def finish(pieces):
        return join(swap(pieces, height_count), me_array).reshape(shape)

    value_pieces = total(
        dv_own, lax.ppermute(dv_high, "tm", up), lax.ppermute(dv_low, "tm", down)
    )
    key_pieces = total(
        dk_own, lax.ppermute(dk_high, "tm", up), lax.ppermute(dk_low, "tm", down)
    )
    query_grad = finish([dq[slot] for slot in range(height_count)])
    value_grad = finish(value_pieces)
    key_grad = finish(key_pieces)
    return query_grad, key_grad, value_grad


TILE = 384
TW = 1


lowest = -1e30


def extended(cells, sides, width):
    for axis, dim in sides:
        count = lax.axis_size(axis)
        ends = count - 1
        head = lax.slice_in_dim(cells, 0, width, axis=dim)
        tail = lax.slice_in_dim(cells, cells.shape[dim] - width, cells.shape[dim], axis=dim)
        cells = jnp.concatenate(
            [
                lax.ppermute(tail, axis, [(i, (i + 1) % count) for i in range(ends)]),
                cells,
                lax.ppermute(head, axis, [((i + 1) % count, i) for i in range(ends)]),
            ],
            axis=dim,
        )
    return cells


def tile_slice(matrix):
    return matrix.reshape(TILE, -1, HD)


def arrange(live_flags):
    ordering = jnp.argsort(1 - live_flags.astype(jnp.int32), stable=True)
    return (ordering, jnp.sum(live_flags.astype(jnp.int32)))


def key_flags(window, time_index, height_index, time_count, height_count):
    item_index = jnp.arange(TW * 27, dtype=jnp.int32)
    tile_number = item_index // 27
    offset = item_index % 27
    source_time = time_index - (offset // 9 - 1)
    source_height = height_index - (offset // 3 % 3 - 1)
    source_tile = tile_number - (offset % 3 - 1)
    inside = (
        (source_time >= 0)
        & (source_time < time_count)
        & (source_height >= 0)
        & (source_height < height_count)
        & (source_tile >= 0)
        & (source_tile < TW)
    )
    looked = window[
        jnp.clip(source_time, 0, time_count - 1),
        jnp.clip(source_height, 0, height_count - 1),
        jnp.clip(source_tile, 0, TW - 1),
        offset,
    ]
    return inside & (looked == 1)


def online_update(previous, scores, slopes):
    highest = jnp.maximum(previous[0], jnp.max(scores, axis=2))
    factor = jnp.exp(previous[0] - highest)
    weights = jnp.exp(scores - highest[:, :, None])
    return jnp.stack(
        [
            highest,
            previous[1] * factor + jnp.sum(weights, axis=2),
            previous[2] * factor + jnp.sum(weights * slopes, axis=2),
        ]
    )


def pair_scores(query_tile, grad_tile, key_tile, value_tile, scaling):
    scores = (
        jnp.einsum("qhd,khd->hqk", query_tile, key_tile, preferred_element_type=jnp.float32)
        * scaling
    )
    slopes = jnp.einsum("qhd,khd->hqk", grad_tile, value_tile, preferred_element_type=jnp.float32)
    return (scores, slopes)


def query_passes(query_rows, grad_rows, neighbours, ordering, live_count, scaling):
    tokens, features = query_rows.shape
    heads_here = features // HD

    def fetch(item_index):
        tile_number = item_index // 27
        offset = item_index % 27
        column = tile_number + offset % 3 - 1
        fetched = lax.dynamic_slice(
            neighbours, (offset // 9, offset // 3 % 3, column * TILE, 0), (1, 1, TILE, 2 * features)
        )
        fetched = fetched.reshape(TILE, 2, heads_here, HD)
        scores, slopes = pair_scores(
            tile_slice(query_rows), tile_slice(grad_rows), fetched[:, 0], fetched[:, 1], scaling
        )
        return (tile_number, fetched[:, 0], scores, slopes)

    def gather_stats(counter, current):
        tile_number, key_tile, scores, slopes = fetch(ordering[counter])
        renewed = online_update(current, scores, slopes)
        return renewed

    start_state = jnp.zeros((3, heads_here, tokens), jnp.float32).at[0].set(lowest)
    final_state = lax.fori_loop(0, live_count, gather_stats, start_state)
    log_total = final_state[0] + jnp.log(final_state[1])
    mean_slope = final_state[2] / final_state[1]

    def gather_query(counter, running):
        tile_number, key_tile, scores, slopes = fetch(ordering[counter])
        probabilities = jnp.exp(scores - log_total[:, :, None])
        score_grads = (probabilities * (slopes - mean_slope[:, :, None])).astype(jnp.bfloat16)
        update = jnp.einsum(
            "hqk,khd->qhd", score_grads, key_tile, preferred_element_type=jnp.float32
        ).reshape(TILE, features)
        return running + update

    query_sum = lax.fori_loop(
        0, live_count, gather_query, jnp.zeros((tokens, features), jnp.float32)
    )
    return (log_total, mean_slope, query_sum)


def key_fetch(item_index, key_rows, value_rows, query_rim, scaling):
    features = key_rows.shape[1]
    heads_here = features // HD
    tile_number = item_index // 27
    offset = item_index % 27
    time_slot = 2 - offset // 9
    height_slot = 2 - offset // 3 % 3
    source = tile_number - offset % 3 + 1
    fetched = lax.dynamic_slice(
        query_rim, (time_slot, height_slot, source * TILE, 0), (1, 1, TILE, 2 * features)
    )
    fetched = fetched.reshape(TILE, 2, heads_here, HD)
    key_tile = tile_slice(key_rows)
    value_tile = tile_slice(value_rows)
    scores, slopes = pair_scores(fetched[:, 0], fetched[:, 1], key_tile, value_tile, scaling)
    return (
        tile_number,
        time_slot,
        height_slot,
        source,
        fetched[:, 0],
        fetched[:, 1],
        key_tile,
        scores,
        slopes,
    )


def owner_grads(key_rows, value_rows, query_rim, stats_rim, ordering, live_count, scaling):
    tokens, features = key_rows.shape
    heads_here = features // HD

    def gather_grads(counter, carried):
        key_sum, value_sum, query_sum = carried
        fetched = key_fetch(ordering[counter], key_rows, value_rows, query_rim, scaling)
        (
            tile_number,
            time_slot,
            height_slot,
            source,
            query_tile,
            grad_tile,
            key_tile,
            scores,
            slopes,
        ) = fetched
        statistics = lax.dynamic_slice(
            stats_rim, (time_slot, height_slot, 0, source * TILE), (1, 1, 2 * heads_here, TILE)
        ).reshape(2, heads_here, TILE)
        probabilities = jnp.exp(scores - statistics[0][:, :, None])
        score_grads = (probabilities * (slopes - statistics[1][:, :, None])).astype(jnp.bfloat16)
        value_part = jnp.einsum(
            "hqk,qhd->khd",
            probabilities.astype(jnp.bfloat16),
            grad_tile,
            preferred_element_type=jnp.float32,
        ).reshape(TILE, features)
        key_part = jnp.einsum(
            "hqk,qhd->khd", score_grads, query_tile, preferred_element_type=jnp.float32
        ).reshape(TILE, features)
        key_sum = key_sum + key_part
        value_sum = value_sum + value_part
        return (key_sum, value_sum, query_sum)

    query_start = jnp.zeros((1,), jnp.float32)
    start_sums = (
        jnp.zeros((tokens, features), jnp.float32),
        jnp.zeros((tokens, features), jnp.float32),
        query_start,
    )
    return lax.fori_loop(0, live_count, gather_grads, start_sums)


def body(grad_output, out_weight, queries, key_states, value_states, window):
    tokens = queries.shape[2]
    features = queries.shape[3]
    heads_here = features // HD
    scaling = HD ** (-0.5)
    grad_rows = grad_output.reshape(tokens, grad_output.shape[3])
    grad_columns = lax.psum_scatter(
        lax.dot_general(
            out_weight, grad_rows, (((1,), (1,)), ((), ())), preferred_element_type=jnp.float32
        ).astype(jnp.bfloat16),
        "heads",
        scatter_dimension=0,
        tiled=True,
    )
    grad_tokens = grad_columns.T
    query_rows = queries.reshape(tokens, features)
    key_rows = key_states.reshape(tokens, features)
    value_rows = value_states.reshape(tokens, features)
    time_index = lax.axis_index("tm")
    height_index = lax.axis_index("height")
    time_count = lax.axis_size("tm")
    height_count = lax.axis_size("height")
    key_order, key_count = arrange(
        key_flags(window, time_index, height_index, time_count, height_count)
    )
    paired = jnp.concatenate([query_rows, grad_tokens], axis=1).reshape(1, 1, tokens, 2 * features)
    query_rim = extended(paired, (("tm", 0), ("height", 1)), 1)
    own_flags = (
        lax.dynamic_slice(window, (time_index, height_index, 0, 0), (1, 1, TW, 27)).reshape(-1) == 1
    )
    own_order, own_count = arrange(own_flags)
    stacked = jnp.concatenate([key_states, value_states], axis=3)
    key_rim = extended(stacked, (("tm", 0), ("height", 1)), 1)
    log_total, mean_slope, query_sum = query_passes(
        query_rows, grad_tokens, key_rim, own_order, own_count, scaling
    )
    statistics = jnp.concatenate([log_total, mean_slope], axis=0).reshape(
        1, 1, 2 * heads_here, tokens
    )
    stats_rim = extended(statistics, (("tm", 0), ("height", 1)), 1)
    key_sum, value_sum, unused = owner_grads(
        key_rows, value_rows, query_rim, stats_rim, key_order, key_count, scaling
    )
    shape = (1, 1, tokens, features)
    query_grad = (scaling * query_sum).astype(jnp.bfloat16).reshape(shape)
    key_grad = (scaling * key_sum).astype(jnp.bfloat16).reshape(shape)
    value_grad = value_sum.astype(jnp.bfloat16).reshape(shape)
    return (query_grad, key_grad, value_grad)


def fits(mesh):
    height, heads = mesh.shape["height"], mesh.shape["heads"]

    def chosen(grad_output, out_weight, queries, key_states, value_states, window):
        features = queries.shape[3]
        power = height & (height - 1) == 0
        fast = heads == 2 and power and features % (height * HD) == 0 and window.shape[2] == 1
        plan = fast_body if fast else body
        return plan(grad_output, out_weight, queries, key_states, value_states, window)

    return chosen


def solution(mesh):
    return jax.shard_map(
        fits(mesh),
        mesh=mesh,
        in_specs=(
            P("tm", "height", None, "heads"),
            P(None, "heads"),
            P("tm", "height", None, "heads"),
            P("tm", "height", None, "heads"),
            P("tm", "height", None, "heads"),
            P(),
        ),
        out_specs=(
            P("tm", "height", None, "heads"),
            P("tm", "height", None, "heads"),
            P("tm", "height", None, "heads"),
        ),
        check_vma=False,
    )
```

```python
import functools

import jax
import jax.numpy as jnp
from jax import lax
from jax.experimental import pallas as pl
from jax.experimental.pallas import tpu as pltpu
from jax.sharding import PartitionSpec as P


HD = 128
LOG2E = 1.4426950408889634
NT = (((1,), (1,)), ((), ()))
TN = (((0,), (0,)), ((), ()))
CHUNK = 192
BF16 = jnp.bfloat16
F32 = jnp.float32


def params(limit=56 << 20):
    return pltpu.CompilerParams(vmem_limit_bytes=limit)


def vmem():
    return pl.BlockSpec(memory_space=pltpu.VMEM)


def smem():
    return pl.BlockSpec(memory_space=pltpu.SMEM)


def hbm():
    return pl.BlockSpec(memory_space=pltpu.HBM)


def cost(moved, flops=0, transcendentals=0):
    return pl.CostEstimate(
        flops=int(flops), transcendentals=int(transcendentals), bytes_accessed=int(moved)
    )


def shaped(shape, kind=BF16):
    return jax.ShapeDtypeStruct(shape, kind)


def run_copies(copies):
    for copy in copies:
        copy.start()
    for copy in copies:
        copy.wait()


def split_kernel(pieces, group, position, key, value, query, *outs):
    me = position[1]
    for slot in range(pieces):
        first = pl.multiple_of((me ^ slot) * group * HD, group * HD)
        for n in range(group):
            columns = pl.ds(first + n * HD, HD)
            outs[n * pieces + slot][0] = key[:, columns]
            outs[n * pieces + slot][1] = value[:, columns]
        outs[group * pieces + slot][0] = query[:, pl.ds(first, group * HD)]


def split(key, value, query, position, pieces, group):
    rows = key.shape[0]
    flat = pl.pallas_call(
        functools.partial(split_kernel, pieces, group),
        out_shape=[shaped((2, rows, HD))] * (group * pieces)
        + [shaped((1, rows, group * HD))] * pieces,
        in_specs=[smem()] + [vmem()] * 3,
        out_specs=[vmem()] * ((group + 1) * pieces),
        name="split_heads",
        cost_estimate=cost(12 * key.size),
    )(position, key, value, query)
    return [flat[i * pieces : (i + 1) * pieces] for i in range(group + 1)]


def join_kernel(pieces, group, position, *refs):
    query_out, key_out, value_out = refs[-3:]
    me = position[1]
    for slot in range(pieces):
        first = pl.multiple_of((me ^ slot) * group * HD, group * HD)
        for n in range(group):
            columns = pl.ds(first + n * HD, HD)
            query_out[:, columns] = refs[slot][n]
            key_out[:, columns] = refs[(n + 1) * pieces + slot][0]
            value_out[:, columns] = refs[(n + 1) * pieces + slot][1]


def join(query_pieces, kv_pieces, position):
    pieces = len(query_pieces)
    group, rows = len(kv_pieces), query_pieces[0].shape[1]
    flat = list(query_pieces) + [piece for part in kv_pieces for piece in part]
    return pl.pallas_call(
        functools.partial(join_kernel, pieces, group),
        out_shape=[shaped((rows, group * pieces * HD))] * 3,
        in_specs=[smem()] + [vmem()] * len(flat),
        out_specs=[vmem()] * 3,
        name="join_heads",
        cost_estimate=cost(12 * rows * group * pieces * HD),
    )(position, *flat)


def swap(pieces):
    count = len(pieces)
    swapped = [pieces[0]]
    for slot in range(1, count):
        swapped.append(lax.ppermute(pieces[slot], "height", [(i, i ^ slot) for i in range(count)]))
    return swapped


def exchange(first, second):
    count = lax.axis_size("tm")
    arrived = []
    for parity, block in ((0, first), (1, second)):
        pairs = [(i, i + 1) for i in range(parity, count - 1, 2)]
        arrived.append(
            lax.ppermute(block, "tm", pairs + [(target, source) for source, target in pairs])
        )
    return arrived


def add_kernel(pieces, group, head, position, full, arrived, *refs):
    mine, sem = refs[-2:]
    me, side = position[1], position[2]
    copies = []
    for slot in range(pieces):
        start = ((side * pieces + (me ^ slot)) * group + head) * HD
        rows = pl.ds(pl.multiple_of(start, HD), HD)
        copies.append(pltpu.make_async_copy(full.at[rows], mine.at[slot], sem.at[slot]))
    run_copies(copies)
    for slot in range(pieces):
        refs[slot][...] = (mine[slot].astype(F32) + arrived[me ^ slot].astype(F32)).astype(BF16)


def add_parts(full, arrived, head, group, position):
    pieces, rows, tokens = arrived.shape
    return pl.pallas_call(
        functools.partial(add_kernel, pieces, group, head),
        out_shape=[shaped((rows, tokens))] * pieces,
        in_specs=[smem(), hbm(), vmem()],
        out_specs=[vmem()] * pieces,
        scratch_shapes=[
            pltpu.VMEM((pieces, rows, tokens), BF16),
            pltpu.SemaphoreType.DMA((pieces,)),
        ],
        name="add_parts",
        cost_estimate=cost(6 * arrived.size),
    )(position, full, arrived)


def total_kernel(own_ref, low_ref, high_ref, *outs):
    for slot, out in enumerate(outs):
        out[...] = (
            own_ref[slot].astype(F32) + (low_ref[slot].astype(F32) + high_ref[slot].astype(F32))
        ).astype(BF16)


def total(own, low, high):
    pieces, planes, rows, width = own.shape
    return pl.pallas_call(
        total_kernel,
        out_shape=[shaped((planes, rows, width))] * pieces,
        in_specs=[vmem()] * 3,
        out_specs=[vmem()] * pieces,
        name="total_grads",
        cost_estimate=cost(8 * own.size),
    )(own, low, high)


def attend_kernel(rows_count, head, position, window, *refs):
    q_in, g_in = refs[:rows_count], refs[rows_count : 2 * rows_count]
    kv_in = refs[2 * rows_count : 2 * rows_count + 3]
    earlier = rows_count if head else 0
    dq_in = refs[2 * rows_count + 3 : 2 * rows_count + 3 + earlier]
    rest = refs[2 * rows_count + 3 + earlier :]
    dq_out, kv_out = rest[:rows_count], rest[rows_count : rows_count + 3]
    q_all, g_all, kv_all, acc, kv_low, dq_all, s_buf, d_buf, order, sem = rest[rows_count + 3 :]
    slot = pl.program_id(0)
    tile = q_all.shape[1]
    scaling = HD**-0.5
    factor = scaling * LOG2E
    chunks = [slice(c * CHUNK, (c + 1) * CHUNK) for c in range(tile // CHUNK)]
    time_index, me = position[0], position[1]

    def loads():
        copies = []
        for i in range(rows_count):
            columns = pl.ds(head * HD, HD)
            copies.append(
                pltpu.make_async_copy(q_in[i].at[0, :, columns], q_all.at[i], sem.at[i])
            )
            copies.append(
                pltpu.make_async_copy(g_in[i], g_all.at[i], sem.at[rows_count + i])
            )
            if head:
                copies.append(
                    pltpu.make_async_copy(
                        dq_in[i], dq_all.at[i, pl.ds(0, head)], sem.at[2 * rows_count + 3 + i]
                    )
                )
        for i in range(3):
            part = pl.ds(i * rows_count, rows_count)
            copies.append(
                pltpu.make_async_copy(kv_in[i], kv_all.at[part], sem.at[2 * rows_count + i])
            )
        return copies

    def stores():
        copies = []
        for i in range(3):
            part = pl.ds(i * rows_count, rows_count)
            copies.append(
                pltpu.make_async_copy(kv_low.at[part], kv_out[i], sem.at[2 * rows_count + i])
            )
        for i in range(rows_count):
            copies.append(pltpu.make_async_copy(dq_all.at[i], dq_out[i], sem.at[i]))
        return copies

    @pl.when(slot == 0)
    def _():
        copies = loads()
        for copy in copies:
            copy.start()
        acc[...] = jnp.zeros_like(acc)
        for copy in copies:
            copy.wait()

    row = me ^ slot
    odd = time_index % 2
    block = (2 - 2 * odd, 1, 2 * odd)
    count = jnp.int32(0)
    for a in range(3):
        for b in range(3):
            order[count] = block[a] * rows_count + ((row + b - 1) ^ me)
            count = count + window[time_index, row, 0, 9 * a + 3 * b + 1]

    query = q_all[slot]
    grad = g_all[slot]

    def scores(i, highest):
        where = order[i]
        for part in chunks:
            s = lax.dot_general(kv_all[where, 0, part, :], query, NT, preferred_element_type=F32)
            s_buf[i, part, :] = s
            highest = jnp.maximum(highest, jnp.max(s.reshape(-1, 8, tile), axis=0))
        return highest

    highest = lax.fori_loop(0, count, scores, jnp.full((8, tile), -1e30, F32))
    highest = jnp.max(highest, axis=0, keepdims=True)

    def sums(i, carried):
        mass, weighted = carried
        where = order[i]
        for part in chunks:
            slopes = jnp.dot(kv_all[where, 1, part, :], grad, preferred_element_type=F32)
            weights = jnp.exp2((s_buf[i, part, :] - highest) * factor)
            s_buf[i, part, :] = weights
            d_buf[i, part, :] = slopes
            mass = mass + jnp.sum(weights.reshape(-1, 8, tile), axis=0)
            weighted = weighted + jnp.sum((weights * slopes).reshape(-1, 8, tile), axis=0)
        return mass, weighted

    zero = jnp.zeros((8, tile), F32)
    mass, weighted = lax.fori_loop(0, count, sums, (zero, zero))
    mass = jnp.sum(mass, axis=0, keepdims=True)
    weighted = jnp.sum(weighted, axis=0, keepdims=True)
    inverse = 1.0 / mass
    delta = weighted * inverse

    def grads(i, query_sum):
        where = order[i]
        for part in chunks:
            weights = s_buf[i, part, :] * inverse
            slopes = (weights * (d_buf[i, part, :] - delta)).astype(BF16)
            weights = weights.astype(BF16)
            acc[where, 1, part, :] += lax.dot_general(
                weights, grad, NT, preferred_element_type=F32
            )
            acc[where, 0, part, :] += jnp.dot(slopes, query, preferred_element_type=F32)
            query_sum = query_sum + lax.dot_general(
                kv_all[where, 0, part, :], slopes, TN, preferred_element_type=F32
            )
        return query_sum

    query_sum = lax.fori_loop(0, count, grads, jnp.zeros((HD, tile), F32))
    dq_all[slot, head] = (scaling * query_sum).T.astype(BF16)

    @pl.when(slot == rows_count - 1)
    def _():
        kv_low[:, 0] = (scaling * acc[:, 0]).astype(BF16)
        kv_low[:, 1] = acc[:, 1].astype(BF16)
        run_copies(stores())


def attend(q_pieces, g_pieces, kv_three, dq_pieces, position, window, head):
    rows_count = len(q_pieces)
    tile = q_pieces[0].shape[1]
    stack = (rows_count, 2, tile, HD)
    flops = rows_count * 3 * 10 * tile * tile * HD
    result = pl.pallas_call(
        functools.partial(attend_kernel, rows_count, head),
        out_shape=[shaped((head + 1, tile, HD))] * rows_count + [shaped(stack)] * 3,
        grid_spec=pltpu.PrefetchScalarGridSpec(
            num_scalar_prefetch=2,
            grid=(rows_count,),
            in_specs=[hbm()] * (2 * rows_count + 3 + len(dq_pieces)),
            out_specs=[hbm()] * (rows_count + 3),
            scratch_shapes=[
                pltpu.VMEM((rows_count, tile, HD), BF16),
                pltpu.VMEM((rows_count, HD, tile), BF16),
                pltpu.VMEM((3 * rows_count, 2, tile, HD), BF16),
                pltpu.VMEM((3 * rows_count, 2, tile, HD), F32),
                pltpu.VMEM((3 * rows_count, 2, tile, HD), BF16),
                pltpu.VMEM((rows_count, head + 1, tile, HD), BF16),
                pltpu.VMEM((9, tile, tile), F32),
                pltpu.VMEM((9, tile, tile), F32),
                pltpu.SMEM((16,), jnp.int32),
                pltpu.SemaphoreType.DMA((3 * rows_count + 3,)),
            ],
        ),
        compiler_params=params(),
        name="attend",
        cost_estimate=cost(28 * tile * HD * rows_count, flops, flops // (10 * HD)),
    )(position, window, *q_pieces, *g_pieces, *kv_three, *dq_pieces)
    return result[:rows_count], result[rows_count:]


def fast_body(grad_output, out_weight, queries, key_states, value_states, window):
    tokens, features = queries.shape[2], queries.shape[3]
    pieces = lax.axis_size("height")
    group = features // (pieces * HD)
    sides = lax.axis_size("heads")
    position = jnp.stack([lax.axis_index(name) for name in ("tm", "height", "heads")])
    position = position.astype(jnp.int32)
    heads = range(group)

    cut = split(
        key_states.reshape(tokens, features),
        value_states.reshape(tokens, features),
        queries.reshape(tokens, features),
        position,
        pieces,
        group,
    )
    kv_pieces = [swap(cut[n]) for n in heads]
    full = lax.dot_general(
        out_weight, grad_output.reshape(tokens, -1), NT, preferred_element_type=F32
    ).astype(BF16)
    other = lax.dynamic_index_in_dim(
        full.reshape(sides, pieces, group, HD, tokens), 1 - position[2], 0, keepdims=False
    )
    arrived = []
    for n in heads:
        arrived.append(lax.ppermute(other[:, n], "heads", [(0, 1), (1, 0)]))
    query_pieces = swap(cut[group])
    grad_pieces = []
    for n in heads:
        parts = add_parts(full, arrived[n], n, group, position)
        grad_pieces.append(swap(parts))
    three = []
    for n in heads:
        stack = jnp.stack(kv_pieces[n])
        near, far = exchange(stack, stack)
        three.append([near, stack, far])
    dq, back = [], []
    for n in heads:
        dq, partials = attend(query_pieces, grad_pieces[n], three[n], dq, position, window, n)
        near, far = exchange(partials[0], partials[2])
        sums = total(partials[1], near, far)
        back.append(swap(sums))
    outs = join(swap(dq), back, position)
    return tuple(out.reshape(1, 1, tokens, features) for out in outs)


TILE = 384
TW = 1


lowest = -1e30


def extended(cells, sides, width):
    for axis, dim in sides:
        count = lax.axis_size(axis)
        ends = count - 1
        head = lax.slice_in_dim(cells, 0, width, axis=dim)
        tail = lax.slice_in_dim(cells, cells.shape[dim] - width, cells.shape[dim], axis=dim)
        cells = jnp.concatenate(
            [
                lax.ppermute(tail, axis, [(i, (i + 1) % count) for i in range(ends)]),
                cells,
                lax.ppermute(head, axis, [((i + 1) % count, i) for i in range(ends)]),
            ],
            axis=dim,
        )
    return cells


def tile_slice(matrix):
    return matrix.reshape(TILE, -1, HD)


def arrange(live_flags):
    ordering = jnp.argsort(1 - live_flags.astype(jnp.int32), stable=True)
    return (ordering, jnp.sum(live_flags.astype(jnp.int32)))


def key_flags(window, time_index, height_index, time_count, height_count):
    item_index = jnp.arange(TW * 27, dtype=jnp.int32)
    tile_number = item_index // 27
    offset = item_index % 27
    source_time = time_index - (offset // 9 - 1)
    source_height = height_index - (offset // 3 % 3 - 1)
    source_tile = tile_number - (offset % 3 - 1)
    inside = (
        (source_time >= 0)
        & (source_time < time_count)
        & (source_height >= 0)
        & (source_height < height_count)
        & (source_tile >= 0)
        & (source_tile < TW)
    )
    looked = window[
        jnp.clip(source_time, 0, time_count - 1),
        jnp.clip(source_height, 0, height_count - 1),
        jnp.clip(source_tile, 0, TW - 1),
        offset,
    ]
    return inside & (looked == 1)


def online_update(previous, scores, slopes):
    highest = jnp.maximum(previous[0], jnp.max(scores, axis=2))
    factor = jnp.exp(previous[0] - highest)
    weights = jnp.exp(scores - highest[:, :, None])
    return jnp.stack(
        [
            highest,
            previous[1] * factor + jnp.sum(weights, axis=2),
            previous[2] * factor + jnp.sum(weights * slopes, axis=2),
        ]
    )


def pair_scores(query_tile, grad_tile, key_tile, value_tile, scaling):
    scores = (
        jnp.einsum("qhd,khd->hqk", query_tile, key_tile, preferred_element_type=jnp.float32)
        * scaling
    )
    slopes = jnp.einsum("qhd,khd->hqk", grad_tile, value_tile, preferred_element_type=jnp.float32)
    return (scores, slopes)


def query_passes(query_rows, grad_rows, neighbours, ordering, live_count, scaling):
    tokens, features = query_rows.shape
    heads_here = features // HD

    def fetch(item_index):
        tile_number = item_index // 27
        offset = item_index % 27
        column = tile_number + offset % 3 - 1
        fetched = lax.dynamic_slice(
            neighbours, (offset // 9, offset // 3 % 3, column * TILE, 0), (1, 1, TILE, 2 * features)
        )
        fetched = fetched.reshape(TILE, 2, heads_here, HD)
        scores, slopes = pair_scores(
            tile_slice(query_rows), tile_slice(grad_rows), fetched[:, 0], fetched[:, 1], scaling
        )
        return (tile_number, fetched[:, 0], scores, slopes)

    def gather_stats(counter, current):
        _, _, scores, slopes = fetch(ordering[counter])
        renewed = online_update(current, scores, slopes)
        return renewed

    start_state = jnp.zeros((3, heads_here, tokens), jnp.float32).at[0].set(lowest)
    final_state = lax.fori_loop(0, live_count, gather_stats, start_state)
    log_total = final_state[0] + jnp.log(final_state[1])
    mean_slope = final_state[2] / final_state[1]

    def gather_query(counter, running):
        _, key_tile, scores, slopes = fetch(ordering[counter])
        probabilities = jnp.exp(scores - log_total[:, :, None])
        score_grads = (probabilities * (slopes - mean_slope[:, :, None])).astype(jnp.bfloat16)
        update = jnp.einsum(
            "hqk,khd->qhd", score_grads, key_tile, preferred_element_type=jnp.float32
        ).reshape(TILE, features)
        return running + update

    query_sum = lax.fori_loop(
        0, live_count, gather_query, jnp.zeros((tokens, features), jnp.float32)
    )
    return (log_total, mean_slope, query_sum)


def key_fetch(item_index, key_rows, value_rows, query_rim, scaling):
    features = key_rows.shape[1]
    heads_here = features // HD
    tile_number = item_index // 27
    offset = item_index % 27
    time_slot = 2 - offset // 9
    height_slot = 2 - offset // 3 % 3
    source = tile_number - offset % 3 + 1
    fetched = lax.dynamic_slice(
        query_rim, (time_slot, height_slot, source * TILE, 0), (1, 1, TILE, 2 * features)
    )
    fetched = fetched.reshape(TILE, 2, heads_here, HD)
    key_tile = tile_slice(key_rows)
    value_tile = tile_slice(value_rows)
    scores, slopes = pair_scores(fetched[:, 0], fetched[:, 1], key_tile, value_tile, scaling)
    return (
        tile_number,
        time_slot,
        height_slot,
        source,
        fetched[:, 0],
        fetched[:, 1],
        key_tile,
        scores,
        slopes,
    )


def owner_grads(key_rows, value_rows, query_rim, stats_rim, ordering, live_count, scaling):
    tokens, features = key_rows.shape
    heads_here = features // HD

    def gather_grads(counter, carried):
        key_sum, value_sum, query_sum = carried
        fetched = key_fetch(ordering[counter], key_rows, value_rows, query_rim, scaling)
        (_, time_slot, height_slot, source, query_tile, grad_tile, _, scores, slopes) = fetched
        statistics = lax.dynamic_slice(
            stats_rim, (time_slot, height_slot, 0, source * TILE), (1, 1, 2 * heads_here, TILE)
        ).reshape(2, heads_here, TILE)
        probabilities = jnp.exp(scores - statistics[0][:, :, None])
        score_grads = (probabilities * (slopes - statistics[1][:, :, None])).astype(jnp.bfloat16)
        value_part = jnp.einsum(
            "hqk,qhd->khd",
            probabilities.astype(jnp.bfloat16),
            grad_tile,
            preferred_element_type=jnp.float32,
        ).reshape(TILE, features)
        key_part = jnp.einsum(
            "hqk,qhd->khd", score_grads, query_tile, preferred_element_type=jnp.float32
        ).reshape(TILE, features)
        key_sum = key_sum + key_part
        value_sum = value_sum + value_part
        return (key_sum, value_sum, query_sum)

    query_start = jnp.zeros((1,), jnp.float32)
    start_sums = (
        jnp.zeros((tokens, features), jnp.float32),
        jnp.zeros((tokens, features), jnp.float32),
        query_start,
    )
    return lax.fori_loop(0, live_count, gather_grads, start_sums)


def body(grad_output, out_weight, queries, key_states, value_states, window):
    tokens = queries.shape[2]
    features = queries.shape[3]
    heads_here = features // HD
    scaling = HD ** (-0.5)
    grad_rows = grad_output.reshape(tokens, grad_output.shape[3])
    grad_columns = lax.psum_scatter(
        lax.dot_general(
            out_weight, grad_rows, (((1,), (1,)), ((), ())), preferred_element_type=jnp.float32
        ).astype(jnp.bfloat16),
        "heads",
        scatter_dimension=0,
        tiled=True,
    )
    grad_tokens = grad_columns.T
    query_rows = queries.reshape(tokens, features)
    key_rows = key_states.reshape(tokens, features)
    value_rows = value_states.reshape(tokens, features)
    time_index = lax.axis_index("tm")
    height_index = lax.axis_index("height")
    time_count = lax.axis_size("tm")
    height_count = lax.axis_size("height")
    key_order, key_count = arrange(
        key_flags(window, time_index, height_index, time_count, height_count)
    )
    paired = jnp.concatenate([query_rows, grad_tokens], axis=1).reshape(1, 1, tokens, 2 * features)
    query_rim = extended(paired, (("tm", 0), ("height", 1)), 1)
    own_flags = (
        lax.dynamic_slice(window, (time_index, height_index, 0, 0), (1, 1, TW, 27)).reshape(-1) == 1
    )
    own_order, own_count = arrange(own_flags)
    stacked = jnp.concatenate([key_states, value_states], axis=3)
    key_rim = extended(stacked, (("tm", 0), ("height", 1)), 1)
    log_total, mean_slope, query_sum = query_passes(
        query_rows, grad_tokens, key_rim, own_order, own_count, scaling
    )
    statistics = jnp.concatenate([log_total, mean_slope], axis=0).reshape(
        1, 1, 2 * heads_here, tokens
    )
    stats_rim = extended(statistics, (("tm", 0), ("height", 1)), 1)
    key_sum, value_sum, _ = owner_grads(
        key_rows, value_rows, query_rim, stats_rim, key_order, key_count, scaling
    )
    shape = (1, 1, tokens, features)
    query_grad = (scaling * query_sum).astype(jnp.bfloat16).reshape(shape)
    key_grad = (scaling * key_sum).astype(jnp.bfloat16).reshape(shape)
    value_grad = value_sum.astype(jnp.bfloat16).reshape(shape)
    return (query_grad, key_grad, value_grad)


def fits(mesh):
    height, heads = mesh.shape["height"], mesh.shape["heads"]

    def chosen(grad_output, out_weight, queries, key_states, value_states, window):
        features = queries.shape[3]
        power = height & (height - 1) == 0
        fast = heads == 2 and power and features % (height * HD) == 0 and window.shape[2] == 1
        fast = fast and features == 2 * height * HD
        plan = fast_body if fast else body
        return plan(grad_output, out_weight, queries, key_states, value_states, window)

    return chosen


def solution(mesh):
    return jax.shard_map(
        fits(mesh),
        mesh=mesh,
        in_specs=(
            P("tm", "height", None, "heads"),
            P(None, "heads"),
            P("tm", "height", None, "heads"),
            P("tm", "height", None, "heads"),
            P("tm", "height", None, "heads"),
            P(),
        ),
        out_specs=(
            P("tm", "height", None, "heads"),
            P("tm", "height", None, "heads"),
            P("tm", "height", None, "heads"),
        ),
        check_vma=False,
    )
```
